32 devices in a mesh: prow: 4 (over z), pcol: 8 (over y, x, core).
Axes of the slice: x: 2, y: 2, z: 4, core: 2. Of those that a mesh axis runs over, the one named last changes fastest.
Arguments:
- matrix: float32 [6, 4, 256, 3, 8, 256], P(None, 'prow', None, None, 'pcol'), may hold values from -6 to 6
- row_order: int32 [6144], replicated, may hold values from 0 to 6143, as said below
- inverses: float32 [4, 256, 256], replicated, may hold values from -0.0234375 to 0.0234375
- lower_fill: int32 [4, 24], replicated, may hold values 0 or 1
- upper_fill: int32 [4, 24], replicated, may hold values 0 or 1
Outputs:
- factored: float32 [6, 4, 256, 3, 8, 256], P(None, 'prow', None, None, 'pcol')
The draws below stay inside these ranges and needn't reach their ends.
Inputs may be any that keep to these rules, and one draw needn't show every extreme that they name: row_order is a permutation of the rows; of the rows whose block row index is congruent to p modulo the number of indices of prow, exactly 6 * 256 divided by that number go to rows whose block row index is congruent to s, for every p and s.
All inputs are finite; a program needn't handle non-finite values.
Results may differ from the reference program's by a relative error of at most 0.0002.
Values sent between devices are 32-bit elements; how exact they have to be, the bound alone decides.
A program may use at most 128 MiB of HBM per device.

```python
import jax
import jax.numpy as jnp
from jax import lax

B = 256
CB = 3
PANELS = 4
RB = 6
NB = 24
N_PROW = 4
N_PCOL = 8


def draw_row_order(key, part):
    local_rows = RB * B
    share = local_rows // N_PROW
    offsets = jnp.arange(local_rows, dtype=jnp.int32)
    owners = jnp.arange(N_PROW, dtype=jnp.int32)
    rows = (offsets[None, :] // B * N_PROW + owners[:, None]) * B + offsets[None, :] % B
    first, second = jax.random.split(jax.random.fold_in(key, 11))

    def shuffle(subkey):
        return jax.vmap(lambda single: jax.random.permutation(single, local_rows))(jax.random.split(subkey, N_PROW))
    sources = jnp.take_along_axis(rows, shuffle(first), 1).reshape(N_PROW, N_PROW, share)
    targets = jnp.take_along_axis(rows, shuffle(second), 1).reshape(N_PROW, N_PROW, share)
    moved = jnp.transpose(targets, (1, 0, 2)).reshape(-1)
    return jnp.zeros((NB * B,), jnp.int32).at[sources.reshape(-1)].set(moved)


def set_ends(values, stream_key, least, top_value):
    dims = values.shape
    place = [jax.random.randint(jax.random.fold_in(stream_key, axis), (), 0, dims[axis]) for axis in range(len(dims))]
    values = values.at[tuple(place)].set(least)
    longest = dims.index(max(dims))
    place[longest] = (place[longest] + 1) % dims[longest]
    return values.at[tuple(place)].set(top_value)


def shard_levels(rng, extent, cuts, least, top_value):
    level, own = 1.0, jax.random.fold_in(rng, 6)
    for position, shards_of in cuts:
        steps = jnp.exp(jax.random.uniform(jax.random.fold_in(own, position), (shards_of,), jnp.float32, least / len(cuts), top_value / len(cuts)))
        level = level * jnp.repeat(steps, extent[position] // shards_of).reshape([-1 if axis == position else 1 for axis in range(len(extent))])
    return level


def bell_draw(own_key, shape, spread, reach, pieces=(), kind=jnp.bfloat16):
    factor_of = shard_levels(own_key, shape, pieces, -0.22, 0.18) if pieces else 1.0
    entries = jax.random.normal(own_key, shape, jnp.float32) * spread * factor_of
    return jnp.minimum(jnp.maximum(entries, -reach), reach).astype(kind)


def setup_inputs(seed: int = 0) -> dict:
    streams_of = jax.random.split(jax.random.key(seed), 6)
    matrix = bell_draw(streams_of[0], (RB, N_PROW, B, CB, N_PCOL, B), 1.0, 6.0, ((1, 4), (4, 8)), jnp.float32)
    row_order = draw_row_order(jax.random.fold_in(streams_of[5], 71), 0)
    inverses = bell_draw(streams_of[2], (PANELS, B, B), (B * B) ** -0.5, 0.0234375, (), jnp.float32)
    lower_fill = set_ends((jax.random.randint(streams_of[3], (PANELS, NB), 0, 4) < 3).astype(jnp.int32), jax.random.fold_in(streams_of[3], 1), 0, 1)
    upper_fill = set_ends((jax.random.randint(streams_of[4], (PANELS, NB), 0, 4) < 3).astype(jnp.int32), jax.random.fold_in(streams_of[4], 1), 0, 1)
    return dict(matrix=matrix, row_order=row_order, inverses=inverses, lower_fill=lower_fill, upper_fill=upper_fill)


def reference(matrix, row_order, inverses, lower_fill, upper_fill):
    order_n = NB * B
    whole = matrix.reshape(order_n, order_n)
    work = jnp.zeros_like(whole).at[row_order].set(whole)
    blocks = jnp.arange(NB, dtype=jnp.int32)
    for k in range(PANELS):
        keep_rows = jnp.repeat(((blocks > k) & (lower_fill[k] == 1)).astype(jnp.float32), B)
        keep_cols = jnp.repeat(((blocks > k) & (upper_fill[k] == 1)).astype(jnp.float32), B)
        column = work[:, k * B:(k + 1) * B]
        lower = jnp.dot(column, inverses[k], precision=lax.Precision.HIGHEST, preferred_element_type=jnp.float32) * keep_rows[:, None]
        upper = work[k * B:(k + 1) * B, :] * keep_cols[None, :]
        start = (k + 1) * B
        update = jnp.dot(lower[start:], upper[:, start:], precision=lax.Precision.HIGHEST, preferred_element_type=jnp.float32)
        work = work.at[start:, start:].add(-update)
        work = work.at[start:, k * B:(k + 1) * B].set(lower[start:])
    return work.reshape(RB, N_PROW, B, CB, N_PCOL, B)
```

```python
import jax
import jax.numpy as jnp
from jax import lax
from jax.sharding import PartitionSpec as P


def mm(a, b):
    return jnp.dot(a, b, precision=lax.Precision.HIGH, preferred_element_type=jnp.float32)


def index_lists(row_order, rows, width, prows, here_row):
    local_rows = rows * width
    blocks = row_order.reshape(rows, prows, width)
    targets = lax.dynamic_index_in_dim(blocks, here_row, 1, keepdims=False).reshape(-1)
    local = jnp.arange(local_rows, dtype=jnp.int32)
    sending = jnp.sort((targets // width % prows) * local_rows + local) % local_rows
    by_source = jnp.transpose(blocks, (1, 0, 2)).reshape(-1)
    dest_local = by_source // width // prows * width + by_source % width
    mine = by_source // width % prows == here_row
    position = jnp.cumsum(mine.astype(jnp.int32)) - 1
    key = jnp.where(mine, dest_local * local_rows + position, local_rows * local_rows)
    taking = jnp.sort(key)[:local_rows] % local_rows
    return sending, taking


def keep_of(fill_row, panel, blocks):
    return (blocks > panel) & (fill_row[blocks] == 1)


def body(matrix, row_order, inverses, lower_fill, upper_fill):
    nrows = matrix.shape[0]
    width = matrix.shape[2]
    ncols = matrix.shape[3]
    prows = lax.axis_size("prow")
    pcols = lax.axis_size("pcol")
    p = lax.axis_index("prow")
    q = lax.axis_index("pcol")
    panels = inverses.shape[0]
    local_rows = nrows * width
    cols = ncols * width
    sending, taking = index_lists(row_order, nrows, width, prows, p)
    work = matrix.reshape(local_rows, cols)
    outgoing = work[sending].reshape(prows, local_rows // prows, cols)
    incoming = lax.all_to_all(outgoing, "prow", split_axis=0, concat_axis=0, tiled=True)
    work = incoming.reshape(local_rows, cols)[taking]
    tops = lax.all_gather(work[:width], "prow", axis=0, tiled=False)[:panels]
    tops = tops.reshape(panels * width, cols)
    column = jnp.concatenate([tops[:, :width], work[:, :width]], axis=0)
    ratio = pcols // panels
    pieces = column.reshape(ratio, -1, width)
    piece = jnp.where(q < panels, pieces[0], 0.0)
    for j in range(1, ratio):
        pairs = [(k, k + panels * j) for k in range(panels)]
        piece = piece + lax.ppermute(pieces[j], "pcol", pairs)
    every = lax.all_gather(piece, "pcol", axis=0, tiled=False)
    every = every.reshape(ratio, panels, piece.shape[0], width)
    columns = [every[:, k].reshape(column.shape) for k in range(panels)]
    row_blocks = jnp.concatenate(
        [jnp.arange(panels, dtype=jnp.int32), jnp.arange(nrows, dtype=jnp.int32) * prows + p]
    )
    col_blocks = jnp.arange(ncols, dtype=jnp.int32) * pcols + q
    corner = panels * width
    lowers, uppers = [], []
    mine = work[:, :width]
    for k in range(panels):
        here = columns[k]
        for m in range(k):
            keep = (upper_fill[m, k] == 1).astype(jnp.float32)
            part = here[m * width : (m + 1) * width] * keep
            here = here - mm(lowers[m], part)
        columns[k] = here
        row_keep = jnp.repeat(keep_of(lower_fill[k], k, row_blocks), width)[:, None]
        lower = jnp.where(row_keep, mm(here, inverses[k]), 0.0)
        lowers.append(lower)
        row = tops[k * width : (k + 1) * width]
        for m in range(k):
            row = row - mm(lower_rows(lowers[m], k, width), uppers[m])
        col_keep = jnp.repeat(keep_of(upper_fill[k], k, col_blocks), width)[None, :]
        uppers.append(jnp.where(col_keep, row, 0.0))
    left = jnp.concatenate([x[corner:] for x in lowers], axis=1)
    out = work - mm(left, jnp.concatenate(uppers, axis=0))
    row_ids = jnp.repeat(row_blocks[panels:], width)[:, None]
    first = out[:, :width]
    for k in range(panels):
        first = jnp.where((q == k) & (row_ids > k), lowers[k][corner:], first)
    out = out.at[:, :width].set(first)
    return out.reshape(nrows, 1, width, ncols, 1, width)


def lower_rows(lower, k, width):
    return lower[k * width : (k + 1) * width]


def solution(mesh):
    in_specs = (P(None, "prow", None, None, "pcol", None), P(), P(), P(), P())
    out_specs = P(None, "prow", None, None, "pcol", None)
    return jax.shard_map(body, mesh=mesh, in_specs=in_specs, out_specs=out_specs, check_vma=False)
```

```python
import functools

import jax
import jax.numpy as jnp
from jax import lax
from jax.experimental import pallas as pl
from jax.experimental.pallas import tpu as pltpu
from jax.sharding import PartitionSpec as P


def mm(a, b):
    return jnp.dot(a, b, precision=lax.Precision.HIGH, preferred_element_type=jnp.float32)


def index_lists(row_order, rows, width, prows, here_row):
    local_rows = rows * width
    blocks = row_order.reshape(rows, prows, width)
    targets = lax.dynamic_index_in_dim(blocks, here_row, 1, keepdims=False).reshape(-1)
    local = jnp.arange(local_rows, dtype=jnp.int32)
    sending = jnp.sort((targets // width % prows) * local_rows + local) % local_rows
    by_source = jnp.transpose(blocks, (1, 0, 2)).reshape(-1)
    dest_local = by_source // width // prows * width + by_source % width
    mine = by_source // width % prows == here_row
    position = jnp.cumsum(mine.astype(jnp.int32)) - 1
    key = jnp.where(mine, dest_local * local_rows + position, local_rows * local_rows)
    taking = jnp.sort(key)[:local_rows] % local_rows
    return sending, taking


def keep_of(fill_row, panel, blocks):
    return (blocks > panel) & (fill_row[blocks] == 1)


def body(matrix, row_order, inverses, lower_fill, upper_fill):
    nrows = matrix.shape[0]
    width = matrix.shape[2]
    ncols = matrix.shape[3]
    prows = lax.axis_size("prow")
    pcols = lax.axis_size("pcol")
    p = lax.axis_index("prow")
    q = lax.axis_index("pcol")
    panels = inverses.shape[0]
    local_rows = nrows * width
    cols = ncols * width
    sending, taking = index_lists(row_order, nrows, width, prows, p)
    work = matrix.reshape(local_rows, cols)
    outgoing = work[sending].reshape(prows, local_rows // prows, cols)
    incoming = lax.all_to_all(outgoing, "prow", split_axis=0, concat_axis=0, tiled=True)
    work = incoming.reshape(local_rows, cols)[taking]
    tops = lax.all_gather(work[:width], "prow", axis=0, tiled=False)[:panels]
    tops = tops.reshape(panels * width, cols)
    column = jnp.concatenate([tops[:, :width], work[:, :width]], axis=0)
    ratio = pcols // panels
    pieces = column.reshape(ratio, -1, width)
    piece = jnp.where(q < panels, pieces[0], 0.0)
    for j in range(1, ratio):
        pairs = [(k, k + panels * j) for k in range(panels)]
        piece = piece + lax.ppermute(pieces[j], "pcol", pairs)
    every = lax.all_gather(piece, "pcol", axis=0, tiled=False)
    every = every.reshape(ratio, panels, piece.shape[0], width)
    columns = [every[:, k].reshape(column.shape) for k in range(panels)]
    row_blocks = jnp.concatenate(
        [jnp.arange(panels, dtype=jnp.int32), jnp.arange(nrows, dtype=jnp.int32) * prows + p]
    )
    col_blocks = jnp.arange(ncols, dtype=jnp.int32) * pcols + q
    corner = panels * width
    lowers, uppers = [], []
    mine = work[:, :width]
    for k in range(panels):
        here = columns[k]
        for m in range(k):
            keep = (upper_fill[m, k] == 1).astype(jnp.float32)
            part = here[m * width : (m + 1) * width] * keep
            here = here - mm(lowers[m], part)
        columns[k] = here
        row_keep = jnp.repeat(keep_of(lower_fill[k], k, row_blocks), width)[:, None]
        lower = jnp.where(row_keep, mm(here, inverses[k]), 0.0)
        lowers.append(lower)
        row = tops[k * width : (k + 1) * width]
        for m in range(k):
            row = row - mm(lower_rows(lowers[m], k, width), uppers[m])
        col_keep = jnp.repeat(keep_of(upper_fill[k], k, col_blocks), width)[None, :]
        uppers.append(jnp.where(col_keep, row, 0.0))
    left = jnp.concatenate([x[corner:] for x in lowers], axis=1)
    out = work - mm(left, jnp.concatenate(uppers, axis=0))
    row_ids = jnp.repeat(row_blocks[panels:], width)[:, None]
    first = out[:, :width]
    for k in range(panels):
        first = jnp.where((q == k) & (row_ids > k), lowers[k][corner:], first)
    out = out.at[:, :width].set(first)
    return out.reshape(nrows, 1, width, ncols, 1, width)


def lower_rows(lower, k, width):
    return lower[k * width : (k + 1) * width]


MESH = pl.DeviceIdType.MESH


def exchange_kernel(
    nrows, width, sending, taking, mat, work, tops, cols,
    send, recv0, recv1, recv2, a2a_send, a2a_recv, ag_send, ag_recv, x_send, x_recv, y_send, y_recv,
    s_send, s_recv, local_sem,
):
    p = lax.axis_index("prow")
    q = lax.axis_index("pcol")
    side, across, core = q // 4, q // 2 % 2, q % 2
    xq = side * 4 + (1 - across) * 2 + core
    yq = (1 - side) * 4 + across * 2 + core
    sq = side * 4 + across * 2 + (1 - core)
    local_rows = nrows * width
    share = local_rows // 4
    top = 2 * width
    size = 4 * width
    others = [((p + t) % 4, q) for t in (2, 1, 3)]

    recv = (recv0, recv1, recv2)
    barrier = pltpu.get_barrier_semaphore()
    for peer in others + [(p, xq), (p, yq), (p, sq)]:
        pl.semaphore_signal(barrier, inc=1, device_id=peer, device_id_type=MESH)
    pl.semaphore_wait(barrier, 6)

    def remote(src, dst, send_sem, recv_sem, peer):
        return pltpu.make_async_remote_copy(
            src_ref=src, dst_ref=dst, send_sem=send_sem, recv_sem=recv_sem,
            device_id=peer, device_id_type=MESH,
        )

    def pick(dst, index, index_base, source, pitch, offset, count):
        unroll = 8

        def group(g, carry):
            for u in range(unroll):
                row = index[index_base + g * unroll + u]
                dst[pl.ds(g * (2 * unroll) + 2 * u, 2), :] = source[
                    pl.ds(row * pitch + offset, 2), :
                ]
            return carry

        lax.fori_loop(0, count // unroll, group, 0)

    def a2a(c, slot):
        peer = others[slot]
        here = recv[c].at[pl.ds(pl.multiple_of(p * (2 * share), 8), 2 * share)]
        return remote(send.at[c, slot], here, a2a_send.at[c, slot], a2a_recv.at[c, slot], peer)

    def scatter_chunk(c):
        for slot in range(3):
            base = others[slot][0] * share
            pick(send.at[c, slot], sending, base, mat, 6, 2 * c, share)
            a2a(c, slot).start()
        mine = recv[c].at[pl.ds(pl.multiple_of(p * (2 * share), 8), 2 * share)]
        pick(mine, sending, p * share, mat, 6, 2 * c, share)

    def collect_chunk(c):
        for slot in range(3):
            a2a(c, slot).wait_recv()
        pick(work.at[c], taking, 0, recv[c], 2, 0, local_rows)

    def top_of(c, owner):
        return tops.at[c, pl.ds(pl.multiple_of(owner * top, 8), top)]

    def gather_own(c):
        own = work.at[c, pl.ds(0, top)]
        copy = pltpu.make_async_copy(own, top_of(c, p), local_sem.at[c])
        copy.start()

        @pl.when(p < 3)
        def _():
            remote(own, top_of(c, p), ag_send.at[c, 0, 0], ag_recv.at[c, 0, 0], (p + 1, q)).start()

        @pl.when(p > 0)
        def _():
            remote(own, top_of(c, p), ag_send.at[c, 1, 0], ag_recv.at[c, 1, 0], (p - 1, q)).start()

    def gather_pass(c, dist):
        for way, step in ((0, 1), (1, -1)):
            owner = p - step * dist
            ahead = p + step

            @pl.when((owner >= 0) & (owner <= 3))
            def _():
                here = top_of(c, owner)
                remote(
                    here, here, ag_send.at[c, way, dist], ag_recv.at[c, way, dist - 1], (p, xq)
                ).wait_recv()

                @pl.when((ahead >= 0) & (ahead <= 3))
                def _():
                    remote(
                        here, here, ag_send.at[c, way, dist],
                        ag_recv.at[c, way, dist], (ahead, q),
                    ).start()

    def gather_sent(c):
        for way, step in ((0, 1), (1, -1)):
            ahead = p + step
            for dist in range(3):
                owner = p - step * dist

                @pl.when((owner >= 0) & (owner <= 3) & (ahead >= 0) & (ahead <= 3))
                def _():
                    here = top_of(c, owner)
                    remote(
                        here, here, ag_send.at[c, way, dist], ag_recv.at[c, way, dist], (p, xq)
                    ).wait_send()

        pltpu.make_async_copy(work.at[c, pl.ds(0, top)], top_of(c, p), local_sem.at[c]).wait()

    straight = across * 2 + core
    cross = (1 - across) * 2 + core
    spots = [4 * top + 0, 4 * top + size, 4 * top + 2 * size, 0, size]

    def place(block, piece):
        return cols.at[block, pl.ds(spots[piece], size)]

    def first_source(piece):
        if piece < 3:
            return work.at[0, pl.ds(piece * size, size)]
        return tops.at[0, pl.ds((piece - 3) * size, size)]

    def to_x(src, piece):
        return remote(src, place(straight, piece), x_send.at[piece], x_recv.at[piece], (p, xq))

    def to_y(src, piece):
        return remote(src, place(straight, piece), y_send.at[piece], y_recv.at[piece], (p, yq))

    def to_s(src, kind, piece):
        block = (straight, cross)[kind]
        return remote(
            src, place(block, piece), s_send.at[kind, piece], s_recv.at[kind, piece], (p, sq)
        )

    def keep_own(piece):
        return pltpu.make_async_copy(
            first_source(piece), place(straight, piece), local_sem.at[3 + piece]
        )

    def column_start(piece):
        @pl.when(side == 0)
        def _():
            src = first_source(piece)
            to_y(src, piece).start()
            to_x(src, piece).start()
            to_s(src, 0, piece).start()
            keep_own(piece).start()

    def column_pass(piece):
        @pl.when(side == 1)
        def _():
            here = place(straight, piece)
            to_y(here, piece).wait_recv()
            to_x(here, piece).start()
            to_s(here, 0, piece).start()

        here = place(cross, piece)
        remote(here, here, x_send.at[piece], x_recv.at[piece], (p, xq)).wait_recv()
        to_s(here, 1, piece).start()

    def column_end(piece):
        for kind in range(2):
            block = (straight, cross)[kind]
            theirs = place(block + 1 - 2 * core, piece)
            remote(
                theirs, theirs, s_send.at[kind, piece], s_recv.at[kind, piece], (p, sq)
            ).wait_recv()
            to_s(theirs, kind, piece).wait_send()
        to_x(place(straight, piece), piece).wait_send()

        @pl.when(side == 0)
        def _():
            to_y(place(straight, piece), piece).wait_send()
            keep_own(piece).wait()

    scatter_chunk(0)
    scatter_chunk(1)
    collect_chunk(0)
    for piece in range(3):
        column_start(piece)
    gather_own(0)
    scatter_chunk(2)
    column_pass(0)
    column_pass(1)
    collect_chunk(1)
    gather_own(1)
    gather_pass(0, 1)
    column_pass(2)
    gather_pass(0, 2)
    gather_pass(0, 3)
    gather_sent(0)
    column_start(3)
    column_start(4)
    collect_chunk(2)
    gather_own(2)
    for dist in (1, 2, 3):
        gather_pass(1, dist)
        gather_pass(2, dist)
    column_pass(3)
    column_pass(4)
    gather_sent(1)
    gather_sent(2)
    for piece in range(5):
        column_end(piece)
    for c in range(3):
        for slot in range(3):
            a2a(c, slot).wait_send()


def exchange(matrix, sending, taking, nrows, width):
    local_rows = nrows * width
    share = local_rows // 4
    dma = pltpu.SemaphoreType.DMA
    vmem = pl.BlockSpec(memory_space=pltpu.VMEM)
    smem = pl.BlockSpec(memory_space=pltpu.SMEM)
    hbm = pl.BlockSpec(memory_space=pl.ANY)
    f32 = jnp.float32
    return pl.pallas_call(
        functools.partial(exchange_kernel, nrows, width),
        out_shape=(
            jax.ShapeDtypeStruct((3, 2 * local_rows, 128), f32),
            jax.ShapeDtypeStruct((3, 8 * width, 128), f32),
            jax.ShapeDtypeStruct((4, 8 * width + 2 * local_rows, 128), f32),
        ),
        in_specs=[smem, smem, vmem],
        out_specs=(vmem, hbm, hbm),
        scratch_shapes=[
            pltpu.VMEM((3, 3, 2 * share, 128), f32),
            pltpu.VMEM((2 * local_rows, 128), f32),
            pltpu.VMEM((2 * local_rows, 128), f32),
            pltpu.VMEM((2 * local_rows, 128), f32),
            dma((3, 3)), dma((3, 3)), dma((3, 2, 4)), dma((3, 2, 4)),
            dma((5,)), dma((5,)), dma((5,)), dma((5,)), dma((2, 5)), dma((2, 5)), dma((8,)),
        ],
        compiler_params=pltpu.CompilerParams(
            collective_id=0, has_side_effects=True, vmem_limit_bytes=60 * 1024 * 1024
        ),
        name="exchange",
    )(sending, taking, matrix)


def halves(x):
    high = x.astype(jnp.bfloat16)
    return high, (x - high.astype(jnp.float32)).astype(jnp.bfloat16)


def dot3(a, b):
    dot = functools.partial(jnp.dot, preferred_element_type=jnp.float32)
    return dot(a[0], b[0]) + (dot(a[0], b[1]) + dot(a[1], b[0]))


def factor_kernel(
    nrows, width, row_keep, col_keep, place_here, work, tops, cols, inv, out, lh, ll, uh, ul, ch, cl
):
    def pairs(ref, lead, start, rows):
        left = ref[lead, pl.ds(start, rows, stride=2), :]
        right = ref[lead, pl.ds(start + 1, rows, stride=2), :]
        return jnp.concatenate([left, right], axis=1)

    def lower_part(start, depth):
        rows = pl.ds(start, width)
        return lh[rows, :depth], ll[rows, :depth]

    corner = 4 * width
    for k in range(4):
        depth = k * width
        inverse = halves(inv[k])

        def finish(h, start, keep):
            low = jnp.where(keep == 1, dot3(halves(h), inverse), 0.0)
            high, rest = halves(low)
            lh[pl.ds(start, width), depth : depth + width] = high
            ll[pl.ds(start, width), depth : depth + width] = rest

        for r in range(4):
            h = pairs(cols, k, 2 * r * width, width)
            take = min(r, k) * width
            if take:
                h = h - dot3(lower_part(r * width, take), (ch[:take, :], cl[:take, :]))
            if r < k:
                high, rest = halves(jnp.where(col_keep[r, 3 + k] == 1, h, 0.0))
                ch[r * width : (r + 1) * width, :] = high
                cl[r * width : (r + 1) * width, :] = rest
            finish(h, r * width, row_keep[k, r])

        def tile(i, carry):
            start = pl.multiple_of(corner + i * width, width)
            h = pairs(cols, k, 2 * start, width)
            if depth:
                h = h - dot3(lower_part(start, depth), (ch[:depth, :], cl[:depth, :]))
            finish(h, start, row_keep[k, 4 + i])
            return carry

        lax.fori_loop(0, nrows, tile, 0)
        for c in range(3):
            span = slice(c * width, (c + 1) * width)
            u = pairs(tops, c, 2 * depth, width)
            if depth:
                u = u - dot3(lower_part(k * width, depth), (uh[:depth, span], ul[:depth, span]))
            high, rest = halves(jnp.where(col_keep[k, c] == 1, u, 0.0))
            uh[depth : depth + width, span] = high
            ul[depth : depth + width, span] = rest

    def update(i, carry):
        start = pl.multiple_of(corner + i * width, width)
        left = lower_part(start, 4 * width)
        for c in range(3):
            span = slice(c * width, (c + 1) * width)
            value = pairs(work, c, 2 * width * i, width) - dot3(left, (uh[:, span], ul[:, span]))
            if c == 0:
                for k in range(4):
                    part = slice(k * width, (k + 1) * width)
                    low = left[0][:, part].astype(jnp.float32) + left[1][:, part].astype(
                        jnp.float32
                    )
                    value = jnp.where(place_here[k, i] == 1, low, value)
            for half in range(2):
                out[pl.ds(i * (6 * width) + 2 * c + half, width, stride=6), :] = value[
                    :, half * 128 : (half + 1) * 128
                ]
        return carry

    lax.fori_loop(0, nrows, update, 0)


def factor(row_keep, col_keep, place_here, work, tops, cols, inverses, nrows, width):
    vmem = pl.BlockSpec(memory_space=pltpu.VMEM)
    smem = pl.BlockSpec(memory_space=pltpu.SMEM)
    rows = (4 + nrows) * width
    bf16 = jnp.bfloat16
    return pl.pallas_call(
        functools.partial(factor_kernel, nrows, width),
        out_shape=jax.ShapeDtypeStruct((nrows * width * 6, 128), jnp.float32),
        in_specs=[smem] * 3 + [vmem] * 4,
        out_specs=vmem,
        scratch_shapes=[
            pltpu.VMEM((rows, 4 * width), bf16), pltpu.VMEM((rows, 4 * width), bf16),
            pltpu.VMEM((4 * width, 3 * width), bf16), pltpu.VMEM((4 * width, 3 * width), bf16),
            pltpu.VMEM((4 * width, width), bf16), pltpu.VMEM((4 * width, width), bf16),
        ],
        compiler_params=pltpu.CompilerParams(vmem_limit_bytes=60 * 1024 * 1024),
        name="factor",
    )(row_keep, col_keep, place_here, work, tops, cols, inverses)


def kernel_body(matrix, row_order, inverses, lower_fill, upper_fill):
    nrows, width = matrix.shape[0], matrix.shape[2]
    p = lax.axis_index("prow")
    q = lax.axis_index("pcol")
    sending, taking = index_lists(row_order, nrows, width, 4, p)
    linear = matrix.reshape(nrows * width * 6, 128)
    work, tops, cols = exchange(linear, sending, taking, nrows, width)
    four = jnp.arange(4, dtype=jnp.int32)
    mine = jnp.arange(nrows, dtype=jnp.int32) * 4 + p
    blocks = jnp.concatenate([four, mine])
    row_keep = ((blocks[None] > four[:, None]) & (lower_fill[:, blocks] == 1)).astype(jnp.int32)
    blocks = jnp.concatenate([jnp.arange(3, dtype=jnp.int32) * 8 + q, four])
    col_keep = ((blocks[None] > four[:, None]) & (upper_fill[:, blocks] == 1)).astype(jnp.int32)
    place_here = ((q == four)[:, None] & (mine[None] > four[:, None])).astype(jnp.int32)
    out = factor(row_keep, col_keep, place_here, work, tops, cols, inverses, nrows, width)
    return out.reshape(matrix.shape)


def solution(mesh):
    in_specs = (P(None, "prow", None, None, "pcol", None), P(), P(), P(), P())
    out_specs = P(None, "prow", None, None, "pcol", None)
    fits = mesh.shape["prow"] == 4 and mesh.shape["pcol"] == 8
    return jax.shard_map(
        kernel_body if fits else body,
        mesh=mesh, in_specs=in_specs, out_specs=out_specs, check_vma=False,
    )
```

```python
import functools

import jax
import jax.numpy as jnp
from jax import lax
from jax.experimental import pallas as pl
from jax.experimental.pallas import tpu as pltpu
from jax.sharding import PartitionSpec as P


def mm(a, b):
    return jnp.dot(a, b, precision=lax.Precision.HIGH, preferred_element_type=jnp.float32)


def index_lists(row_order, rows, width, prows, here_row):
    local_rows = rows * width
    blocks = row_order.reshape(rows, prows, width)
    targets = lax.dynamic_index_in_dim(blocks, here_row, 1, keepdims=False).reshape(-1)
    local = jnp.arange(local_rows, dtype=jnp.int32)
    sending = (targets // width % prows) * local_rows + local
    by_source = jnp.transpose(blocks, (1, 0, 2)).reshape(-1)
    dest_local = by_source // width // prows * width + by_source % width
    mine = by_source // width % prows == here_row
    position = jnp.cumsum(mine.astype(jnp.int32)) - 1
    key = jnp.where(mine, dest_local * local_rows + position, local_rows * local_rows)
    both = jnp.concatenate([sending, prows * local_rows + key])
    both = lax.sort(both, is_stable=False)[: 2 * local_rows] % local_rows
    return both[:local_rows], both[local_rows:]


def keep_of(fill_row, panel, blocks):
    return (blocks > panel) & (fill_row[blocks] == 1)


def body(matrix, row_order, inverses, lower_fill, upper_fill):
    nrows = matrix.shape[0]
    width = matrix.shape[2]
    ncols = matrix.shape[3]
    prows = lax.axis_size("prow")
    pcols = lax.axis_size("pcol")
    p = lax.axis_index("prow")
    q = lax.axis_index("pcol")
    panels = inverses.shape[0]
    local_rows = nrows * width
    cols = ncols * width
    sending, taking = index_lists(row_order, nrows, width, prows, p)
    work = matrix.reshape(local_rows, cols)
    outgoing = work[sending].reshape(prows, local_rows // prows, cols)
    incoming = lax.all_to_all(outgoing, "prow", split_axis=0, concat_axis=0, tiled=True)
    work = incoming.reshape(local_rows, cols)[taking]
    tops = lax.all_gather(work[:width], "prow", axis=0, tiled=False)[:panels]
    tops = tops.reshape(panels * width, cols)
    column = jnp.concatenate([tops[:, :width], work[:, :width]], axis=0)
    ratio = pcols // panels
    pieces = column.reshape(ratio, -1, width)
    piece = jnp.where(q < panels, pieces[0], 0.0)
    for j in range(1, ratio):
        pairs = [(k, k + panels * j) for k in range(panels)]
        piece = piece + lax.ppermute(pieces[j], "pcol", pairs)
    every = lax.all_gather(piece, "pcol", axis=0, tiled=False)
    every = every.reshape(ratio, panels, piece.shape[0], width)
    columns = [every[:, k].reshape(column.shape) for k in range(panels)]
    row_blocks = jnp.concatenate(
        [jnp.arange(panels, dtype=jnp.int32), jnp.arange(nrows, dtype=jnp.int32) * prows + p]
    )
    col_blocks = jnp.arange(ncols, dtype=jnp.int32) * pcols + q
    corner = panels * width
    lowers, uppers = [], []
    mine = work[:, :width]
    for k in range(panels):
        here = columns[k]
        for m in range(k):
            keep = (upper_fill[m, k] == 1).astype(jnp.float32)
            part = here[m * width : (m + 1) * width] * keep
            here = here - mm(lowers[m], part)
        columns[k] = here
        row_keep = jnp.repeat(keep_of(lower_fill[k], k, row_blocks), width)[:, None]
        lower = jnp.where(row_keep, mm(here, inverses[k]), 0.0)
        lowers.append(lower)
        row = tops[k * width : (k + 1) * width]
        for m in range(k):
            row = row - mm(lower_rows(lowers[m], k, width), uppers[m])
        col_keep = jnp.repeat(keep_of(upper_fill[k], k, col_blocks), width)[None, :]
        uppers.append(jnp.where(col_keep, row, 0.0))
    left = jnp.concatenate([x[corner:] for x in lowers], axis=1)
    out = work - mm(left, jnp.concatenate(uppers, axis=0))
    row_ids = jnp.repeat(row_blocks[panels:], width)[:, None]
    first = out[:, :width]
    for k in range(panels):
        first = jnp.where((q == k) & (row_ids > k), lowers[k][corner:], first)
    out = out.at[:, :width].set(first)
    return out.reshape(nrows, 1, width, ncols, 1, width)


def lower_rows(lower, k, width):
    return lower[k * width : (k + 1) * width]


MESH = pl.DeviceIdType.MESH


def exchange_kernel(
    nrows, width, sending, taking, mat, work, tops, cols,
    send, recv0, recv1, recv2, a2a_send, a2a_recv, ag_send, ag_recv, x_send, x_recv, y_send, y_recv,
    s_send, s_recv, local_sem,
):
    p = lax.axis_index("prow")
    q = lax.axis_index("pcol")
    side, across, core = q // 4, q // 2 % 2, q % 2
    xq = side * 4 + (1 - across) * 2 + core
    yq = (1 - side) * 4 + across * 2 + core
    sq = side * 4 + across * 2 + (1 - core)
    local_rows = nrows * width
    share = local_rows // 4
    top = 2 * width
    size = 4 * width
    others = [((p + t) % 4, q) for t in (2, 1, 3)]

    recv = (recv0, recv1, recv2)
    barrier = pltpu.get_barrier_semaphore()
    for peer in others + [(p, xq), (p, yq), (p, sq)]:
        pl.semaphore_signal(barrier, inc=1, device_id=peer, device_id_type=MESH)
    pl.semaphore_wait(barrier, 6)

    def remote(src, dst, send_sem, recv_sem, peer):
        return pltpu.make_async_remote_copy(
            src_ref=src, dst_ref=dst, send_sem=send_sem, recv_sem=recv_sem,
            device_id=peer, device_id_type=MESH,
        )

    def pick(dst, index, index_base, source, pitch, offset, count):
        unroll = 8

        def group(g, carry):
            for u in range(unroll):
                row = index[index_base + g * unroll + u]
                dst[pl.ds(g * (2 * unroll) + 2 * u, 2), :] = source[
                    pl.ds(row * pitch + offset, 2), :
                ]
            return carry

        lax.fori_loop(0, count // unroll, group, 0)

    def a2a(c, slot):
        peer = others[slot]
        here = recv[c].at[pl.ds(pl.multiple_of(p * (2 * share), 8), 2 * share)]
        return remote(send.at[c, slot], here, a2a_send.at[c, slot], a2a_recv.at[c, slot], peer)

    def scatter_part(c, slots):
        for slot in slots:
            base = others[slot][0] * share
            pick(send.at[c, slot], sending, base, mat, 6, 2 * c, share)
            a2a(c, slot).start()
        if 2 in slots:
            mine = recv[c].at[pl.ds(pl.multiple_of(p * (2 * share), 8), 2 * share)]
            pick(mine, sending, p * share, mat, 6, 2 * c, share)

    def collect_chunk(c):
        for slot in range(3):
            a2a(c, slot).wait_recv()
        pick(work.at[c], taking, 0, recv[c], 2, 0, local_rows)

    def top_of(c, owner):
        return tops.at[c, pl.ds(pl.multiple_of(owner * top, 8), top)]

    def gather_own(c):
        own = work.at[c, pl.ds(0, top)]
        copy = pltpu.make_async_copy(own, top_of(c, p), local_sem.at[c])
        copy.start()

        @pl.when(p < 3)
        def _():
            remote(own, top_of(c, p), ag_send.at[c, 0, 0], ag_recv.at[c, 0, 0], (p + 1, q)).start()

        @pl.when(p > 0)
        def _():
            remote(own, top_of(c, p), ag_send.at[c, 1, 0], ag_recv.at[c, 1, 0], (p - 1, q)).start()

    def gather_pass(c, dist):
        for way, step in ((0, 1), (1, -1)):
            owner = p - step * dist
            ahead = p + step

            @pl.when((owner >= 0) & (owner <= 3))
            def _():
                here = top_of(c, owner)
                remote(
                    here, here, ag_send.at[c, way, dist], ag_recv.at[c, way, dist - 1], (p, xq)
                ).wait_recv()

                @pl.when((ahead >= 0) & (ahead <= 3))
                def _():
                    remote(
                        here, here, ag_send.at[c, way, dist],
                        ag_recv.at[c, way, dist], (ahead, q),
                    ).start()

    def gather_sent(c):
        for way, step in ((0, 1), (1, -1)):
            ahead = p + step
            for dist in range(3):
                owner = p - step * dist

                @pl.when((owner >= 0) & (owner <= 3) & (ahead >= 0) & (ahead <= 3))
                def _():
                    here = top_of(c, owner)
                    remote(
                        here, here, ag_send.at[c, way, dist], ag_recv.at[c, way, dist], (p, xq)
                    ).wait_send()

    def gather_kept(c):
        pltpu.make_async_copy(work.at[c, pl.ds(0, top)], top_of(c, p), local_sem.at[c]).wait()

    straight = across * 2 + core
    cross = (1 - across) * 2 + core
    spots = [4 * top + 0, 4 * top + size, 4 * top + 2 * size, 0, size]

    def place(block, piece):
        return cols.at[block, pl.ds(spots[piece], size)]

    def first_source(piece):
        if piece < 3:
            return work.at[0, pl.ds(piece * size, size)]
        return tops.at[0, pl.ds((piece - 3) * size, size)]

    def to_x(src, piece):
        return remote(src, place(straight, piece), x_send.at[piece], x_recv.at[piece], (p, xq))

    def to_y(src, piece):
        return remote(src, place(straight, piece), y_send.at[piece], y_recv.at[piece], (p, yq))

    def to_s(src, kind, piece):
        block = (straight, cross)[kind]
        return remote(
            src, place(block, piece), s_send.at[kind, piece], s_recv.at[kind, piece], (p, sq)
        )

    def keep_own(piece):
        return pltpu.make_async_copy(
            first_source(piece), place(straight, piece), local_sem.at[3 + piece]
        )

    def column_start(piece):
        @pl.when(side == 0)
        def _():
            src = first_source(piece)
            to_y(src, piece).start()
            to_x(src, piece).start()
            to_s(src, 0, piece).start()
            keep_own(piece).start()

    def column_pass(piece):
        @pl.when(side == 1)
        def _():
            here = place(straight, piece)
            to_y(here, piece).wait_recv()
            to_x(here, piece).start()
            to_s(here, 0, piece).start()

        here = place(cross, piece)
        remote(here, here, x_send.at[piece], x_recv.at[piece], (p, xq)).wait_recv()
        to_s(here, 1, piece).start()

    def column_end(piece):
        for kind in range(2):
            block = (straight, cross)[kind]
            theirs = place(block + 1 - 2 * core, piece)
            remote(
                theirs, theirs, s_send.at[kind, piece], s_recv.at[kind, piece], (p, sq)
            ).wait_recv()
            to_s(theirs, kind, piece).wait_send()
        to_x(place(straight, piece), piece).wait_send()

        @pl.when(side == 0)
        def _():
            to_y(place(straight, piece), piece).wait_send()
            keep_own(piece).wait()

    scatter_part(0, (0, 1, 2))
    scatter_part(1, (0,))
    collect_chunk(0)
    for piece in range(3):
        column_start(piece)
    gather_own(0)
    scatter_part(1, (1, 2))
    column_pass(0)
    gather_pass(0, 1)
    scatter_part(2, (0,))
    column_pass(1)
    gather_pass(0, 2)
    scatter_part(2, (1, 2))
    collect_chunk(1)
    gather_own(1)
    column_pass(2)
    gather_pass(0, 3)
    gather_kept(0)
    column_start(3)
    column_start(4)
    gather_pass(1, 1)
    collect_chunk(2)
    gather_own(2)
    gather_pass(1, 2)
    column_pass(3)
    gather_pass(2, 1)
    gather_pass(1, 3)
    gather_pass(2, 2)
    column_pass(4)
    gather_pass(2, 3)
    gather_kept(1)
    gather_kept(2)
    for c in range(3):
        gather_sent(c)
    for piece in range(5):
        column_end(piece)
    for c in range(3):
        for slot in range(3):
            a2a(c, slot).wait_send()


def exchange(matrix, sending, taking, nrows, width):
    local_rows = nrows * width
    share = local_rows // 4
    dma = pltpu.SemaphoreType.DMA
    vmem = pl.BlockSpec(memory_space=pltpu.VMEM)
    smem = pl.BlockSpec(memory_space=pltpu.SMEM)
    hbm = pl.BlockSpec(memory_space=pl.ANY)
    f32 = jnp.float32
    return pl.pallas_call(
        functools.partial(exchange_kernel, nrows, width),
        out_shape=(
            jax.ShapeDtypeStruct((3, 2 * local_rows, 128), f32),
            jax.ShapeDtypeStruct((3, 8 * width, 128), f32),
            jax.ShapeDtypeStruct((4, 8 * width + 2 * local_rows, 128), f32),
        ),
        in_specs=[smem, smem, vmem],
        out_specs=(vmem, hbm, hbm),
        scratch_shapes=[
            pltpu.VMEM((3, 3, 2 * share, 128), f32),
            pltpu.VMEM((2 * local_rows, 128), f32),
            pltpu.VMEM((2 * local_rows, 128), f32),
            pltpu.VMEM((2 * local_rows, 128), f32),
            dma((3, 3)), dma((3, 3)), dma((3, 2, 4)), dma((3, 2, 4)),
            dma((5,)), dma((5,)), dma((5,)), dma((5,)), dma((2, 5)), dma((2, 5)), dma((8,)),
        ],
        compiler_params=pltpu.CompilerParams(
            collective_id=0, has_side_effects=True, vmem_limit_bytes=60 * 1024 * 1024
        ),
        name="exchange",
    )(sending, taking, matrix)


def halves(x):
    high = x.astype(jnp.bfloat16)
    return high, (x - high.astype(jnp.float32)).astype(jnp.bfloat16)


def left3(x):
    high, rest = halves(x)
    return jnp.concatenate([high, high, rest], axis=1)


def right3(x):
    high, rest = halves(x)
    return jnp.concatenate([high, rest, high], axis=0)


def factor_kernel(
    nrows, width, lower_fill, upper_fill, work, tops, cols, inv, out, l3, u3, c3
):
    p = lax.axis_index("prow")
    q = lax.axis_index("pcol")

    def dot(a, b):
        return jnp.dot(a, b, preferred_element_type=jnp.float32)

    def kept(fill, k, block):
        return (block > k) & (fill[k, block] == 1)

    def pairs(ref, lead, start, rows):
        left = ref[lead, pl.ds(start, rows, stride=2), :]
        right = ref[lead, pl.ds(start + 1, rows, stride=2), :]
        return jnp.concatenate([left, right], axis=1)

    corner = 4 * width
    for k in range(4):
        deep = 3 * k * width
        inverse = right3(inv[k])

        def finish(h, start, keep):
            low = jnp.where(keep, dot(left3(h), inverse), 0.0)
            l3[pl.ds(start, width), deep : deep + 3 * width] = left3(low)

        for r in range(4):
            h = pairs(cols, k, 2 * r * width, width)
            take = 3 * min(r, k) * width
            if take:
                h = h - dot(l3[r * width : (r + 1) * width, :take], c3[:take, :])
            if r < k:
                c3[3 * r * width : 3 * (r + 1) * width, :] = right3(
                    jnp.where(kept(upper_fill, r, k), h, 0.0)
                )
            finish(h, r * width, kept(lower_fill, k, r))

        def tile(i, carry):
            start = pl.multiple_of(corner + i * width, width)
            h = pairs(cols, k, 2 * start, width)
            if deep:
                h = h - dot(l3[pl.ds(start, width), :deep], c3[:deep, :])
            finish(h, start, kept(lower_fill, k, i * 4 + p))
            return carry

        lax.fori_loop(0, nrows, tile, 0)
        for c in range(3):
            span = slice(c * width, (c + 1) * width)
            u = pairs(tops, c, 2 * k * width, width)
            if deep:
                u = u - dot(l3[k * width : (k + 1) * width, :deep], u3[:deep, span])
            u3[deep : deep + 3 * width, span] = right3(
                jnp.where(kept(upper_fill, k, c * 8 + q), u, 0.0)
            )

    def update(i, carry):
        start = pl.multiple_of(corner + i * width, width)
        for c in range(3):
            span = slice(c * width, (c + 1) * width)
            value = pairs(work, c, 2 * width * i, width) - dot(
                l3[pl.ds(start, width), :], u3[:, span]
            )
            if c == 0:
                for k in range(4):
                    deep = 3 * k * width
                    high = l3[pl.ds(start, width), deep : deep + width].astype(jnp.float32)
                    rest = l3[pl.ds(start, width), deep + 2 * width : deep + 3 * width]
                    low = high + rest.astype(jnp.float32)
                    value = jnp.where((q == k) & (i * 4 + p > k), low, value)
            for half in range(2):
                out[pl.ds(i * (6 * width) + 2 * c + half, width, stride=6), :] = value[
                    :, half * 128 : (half + 1) * 128
                ]
        return carry

    lax.fori_loop(0, nrows, update, 0)


def factor(lower_fill, upper_fill, work, tops, cols, inverses, nrows, width):
    vmem = pl.BlockSpec(memory_space=pltpu.VMEM)
    smem = pl.BlockSpec(memory_space=pltpu.SMEM)
    rows = (4 + nrows) * width
    bf16 = jnp.bfloat16
    return pl.pallas_call(
        functools.partial(factor_kernel, nrows, width),
        out_shape=jax.ShapeDtypeStruct((nrows * width * 6, 128), jnp.float32),
        in_specs=[smem] * 2 + [vmem] * 4,
        out_specs=vmem,
        scratch_shapes=[
            pltpu.VMEM((rows, 12 * width), bf16),
            pltpu.VMEM((12 * width, 3 * width), bf16),
            pltpu.VMEM((12 * width, width), bf16),
        ],
        compiler_params=pltpu.CompilerParams(vmem_limit_bytes=60 * 1024 * 1024),
        name="factor",
    )(lower_fill, upper_fill, work, tops, cols, inverses)


def kernel_body(matrix, row_order, inverses, lower_fill, upper_fill):
    nrows, width = matrix.shape[0], matrix.shape[2]
    p = lax.axis_index("prow")
    sending, taking = index_lists(row_order, nrows, width, 4, p)
    linear = matrix.reshape(nrows * width * 6, 128)
    work, tops, cols = exchange(linear, sending, taking, nrows, width)
    out = factor(lower_fill, upper_fill, work, tops, cols, inverses, nrows, width)
    return out.reshape(matrix.shape)


def solution(mesh):
    in_specs = (P(None, "prow", None, None, "pcol", None), P(), P(), P(), P())
    out_specs = P(None, "prow", None, None, "pcol", None)
    fits = mesh.shape["prow"] == 4 and mesh.shape["pcol"] == 8
    return jax.shard_map(
        kernel_body if fits else body,
        mesh=mesh, in_specs=in_specs, out_specs=out_specs, check_vma=False,
    )
```

```python
import functools

import jax
import jax.numpy as jnp
from jax import lax
from jax.experimental import pallas as pl
from jax.experimental.pallas import tpu as pltpu
from jax.sharding import PartitionSpec as P


def mm(a, b):
    return jnp.dot(a, b, precision=lax.Precision.HIGH, preferred_element_type=jnp.float32)


def index_lists(row_order, rows, width, prows, here_row):
    local_rows = rows * width
    blocks = row_order.reshape(rows, prows, width)
    targets = lax.dynamic_index_in_dim(blocks, here_row, 1, keepdims=False).reshape(-1)
    local = jnp.arange(local_rows, dtype=jnp.int32)
    sending = (targets // width % prows) * local_rows + local
    by_source = jnp.transpose(blocks, (1, 0, 2)).reshape(-1)
    dest_local = by_source // width // prows * width + by_source % width
    mine = by_source // width % prows == here_row
    position = jnp.cumsum(mine.astype(jnp.int32)) - 1
    key = jnp.where(mine, dest_local * local_rows + position, local_rows * local_rows)
    both = jnp.concatenate([sending, prows * local_rows + key])
    both = lax.sort(both, is_stable=False)[: 2 * local_rows] % local_rows
    return both[:local_rows], both[local_rows:]


def keep_of(fill_row, panel, blocks):
    return (blocks > panel) & (fill_row[blocks] == 1)


def body(matrix, row_order, inverses, lower_fill, upper_fill):
    nrows = matrix.shape[0]
    width = matrix.shape[2]
    ncols = matrix.shape[3]
    prows = lax.axis_size("prow")
    pcols = lax.axis_size("pcol")
    p = lax.axis_index("prow")
    q = lax.axis_index("pcol")
    panels = inverses.shape[0]
    local_rows = nrows * width
    cols = ncols * width
    sending, taking = index_lists(row_order, nrows, width, prows, p)
    work = matrix.reshape(local_rows, cols)
    outgoing = work[sending].reshape(prows, local_rows // prows, cols)
    incoming = lax.all_to_all(outgoing, "prow", split_axis=0, concat_axis=0, tiled=True)
    work = incoming.reshape(local_rows, cols)[taking]
    tops = lax.all_gather(work[:width], "prow", axis=0, tiled=False)[:panels]
    tops = tops.reshape(panels * width, cols)
    column = jnp.concatenate([tops[:, :width], work[:, :width]], axis=0)
    ratio = pcols // panels
    pieces = column.reshape(ratio, -1, width)
    piece = jnp.where(q < panels, pieces[0], 0.0)
    for j in range(1, ratio):
        pairs = [(k, k + panels * j) for k in range(panels)]
        piece = piece + lax.ppermute(pieces[j], "pcol", pairs)
    every = lax.all_gather(piece, "pcol", axis=0, tiled=False)
    every = every.reshape(ratio, panels, piece.shape[0], width)
    columns = [every[:, k].reshape(column.shape) for k in range(panels)]
    row_blocks = jnp.concatenate(
        [jnp.arange(panels, dtype=jnp.int32), jnp.arange(nrows, dtype=jnp.int32) * prows + p]
    )
    col_blocks = jnp.arange(ncols, dtype=jnp.int32) * pcols + q
    corner = panels * width
    lowers, uppers = [], []
    mine = work[:, :width]
    for k in range(panels):
        here = columns[k]
        for m in range(k):
            keep = (upper_fill[m, k] == 1).astype(jnp.float32)
            part = here[m * width : (m + 1) * width] * keep
            here = here - mm(lowers[m], part)
        columns[k] = here
        row_keep = jnp.repeat(keep_of(lower_fill[k], k, row_blocks), width)[:, None]
        lower = jnp.where(row_keep, mm(here, inverses[k]), 0.0)
        lowers.append(lower)
        row = tops[k * width : (k + 1) * width]
        for m in range(k):
            row = row - mm(lower_rows(lowers[m], k, width), uppers[m])
        col_keep = jnp.repeat(keep_of(upper_fill[k], k, col_blocks), width)[None, :]
        uppers.append(jnp.where(col_keep, row, 0.0))
    left = jnp.concatenate([x[corner:] for x in lowers], axis=1)
    out = work - mm(left, jnp.concatenate(uppers, axis=0))
    row_ids = jnp.repeat(row_blocks[panels:], width)[:, None]
    first = out[:, :width]
    for k in range(panels):
        first = jnp.where((q == k) & (row_ids > k), lowers[k][corner:], first)
    out = out.at[:, :width].set(first)
    return out.reshape(nrows, 1, width, ncols, 1, width)


def lower_rows(lower, k, width):
    return lower[k * width : (k + 1) * width]


MESH = pl.DeviceIdType.MESH


def exchange_kernel(
    nrows, width, sending, taking, mat, work, tops, cols,
    send, recv0, recv1, recv2, a2a_send, a2a_recv, ag_send, ag_recv, x_send, x_recv, y_send, y_recv,
    s_send, s_recv, local_sem,
):
    p = lax.axis_index("prow")
    q = lax.axis_index("pcol")
    side, across, core = q // 4, q // 2 % 2, q % 2
    xq = side * 4 + (1 - across) * 2 + core
    yq = (1 - side) * 4 + across * 2 + core
    sq = side * 4 + across * 2 + (1 - core)
    local_rows = nrows * width
    share = local_rows // 4
    top = 2 * width
    size = 4 * width
    others = [((p + t) % 4, q) for t in (2, 1, 3)]

    recv = (recv0, recv1, recv2)
    barrier = pltpu.get_barrier_semaphore()
    for peer in others + [(p, xq), (p, yq), (p, sq)]:
        pl.semaphore_signal(barrier, inc=1, device_id=peer, device_id_type=MESH)
    pl.semaphore_wait(barrier, 6)

    def remote(src, dst, send_sem, recv_sem, peer):
        return pltpu.make_async_remote_copy(
            src_ref=src, dst_ref=dst, send_sem=send_sem, recv_sem=recv_sem,
            device_id=peer, device_id_type=MESH,
        )

    def pick(dst, index, index_base, source, pitch, offset, count):
        unroll = 8

        def group(g, carry):
            for u in range(unroll):
                row = index[index_base + g * unroll + u]
                dst[pl.ds(g * (2 * unroll) + 2 * u, 2), :] = source[
                    pl.ds(row * pitch + offset, 2), :
                ]
            return carry

        lax.fori_loop(0, count // unroll, group, 0)

    def a2a(c, slot):
        peer = others[slot]
        here = recv[c].at[pl.ds(pl.multiple_of(p * (2 * share), 8), 2 * share)]
        return remote(send.at[c, slot], here, a2a_send.at[c, slot], a2a_recv.at[c, slot], peer)

    def scatter_part(c, slots):
        for slot in slots:
            base = others[slot][0] * share
            pick(send.at[c, slot], sending, base, mat, 6, 2 * c, share)
            a2a(c, slot).start()
        if 2 in slots:
            mine = recv[c].at[pl.ds(pl.multiple_of(p * (2 * share), 8), 2 * share)]
            pick(mine, sending, p * share, mat, 6, 2 * c, share)

    def collect_chunk(c):
        for slot in range(3):
            a2a(c, slot).wait_recv()
        pick(work.at[c], taking, 0, recv[c], 2, 0, local_rows)

    def top_of(c, owner):
        return tops.at[c, pl.ds(pl.multiple_of(owner * top, 8), top)]

    def gather_own(c):
        own = work.at[c, pl.ds(0, top)]
        copy = pltpu.make_async_copy(own, top_of(c, p), local_sem.at[c])
        copy.start()

        @pl.when(p < 3)
        def _():
            remote(own, top_of(c, p), ag_send.at[c, 0, 0], ag_recv.at[c, 0, 0], (p + 1, q)).start()

        @pl.when(p > 0)
        def _():
            remote(own, top_of(c, p), ag_send.at[c, 1, 0], ag_recv.at[c, 1, 0], (p - 1, q)).start()

    def gather_pass(c, dist):
        for way, step in ((0, 1), (1, -1)):
            owner = p - step * dist
            ahead = p + step

            @pl.when((owner >= 0) & (owner <= 3))
            def _():
                here = top_of(c, owner)
                remote(
                    here, here, ag_send.at[c, way, dist], ag_recv.at[c, way, dist - 1], (p, xq)
                ).wait_recv()

                @pl.when((ahead >= 0) & (ahead <= 3))
                def _():
                    remote(
                        here, here, ag_send.at[c, way, dist],
                        ag_recv.at[c, way, dist], (ahead, q),
                    ).start()

    def gather_sent(c):
        for way, step in ((0, 1), (1, -1)):
            ahead = p + step
            for dist in range(3):
                owner = p - step * dist

                @pl.when((owner >= 0) & (owner <= 3) & (ahead >= 0) & (ahead <= 3))
                def _():
                    here = top_of(c, owner)
                    remote(
                        here, here, ag_send.at[c, way, dist], ag_recv.at[c, way, dist], (p, xq)
                    ).wait_send()

    def gather_kept(c):
        pltpu.make_async_copy(work.at[c, pl.ds(0, top)], top_of(c, p), local_sem.at[c]).wait()

    straight = across * 2 + core
    cross = (1 - across) * 2 + core
    spots = [4 * top + 0, 4 * top + size, 4 * top + 2 * size, 0, size]

    def place(block, piece):
        return cols.at[block, pl.ds(spots[piece], size)]

    def first_source(piece):
        if piece < 3:
            return work.at[0, pl.ds(piece * size, size)]
        return tops.at[0, pl.ds((piece - 3) * size, size)]

    def to_x(src, piece):
        return remote(src, place(straight, piece), x_send.at[piece], x_recv.at[piece], (p, xq))

    def to_y(src, piece):
        return remote(src, place(straight, piece), y_send.at[piece], y_recv.at[piece], (p, yq))

    def to_s(src, kind, piece):
        block = (straight, cross)[kind]
        return remote(
            src, place(block, piece), s_send.at[kind, piece], s_recv.at[kind, piece], (p, sq)
        )

    def keep_own(piece):
        return pltpu.make_async_copy(
            first_source(piece), place(straight, piece), local_sem.at[3 + piece]
        )

    def column_start(piece):
        @pl.when(side == 0)
        def _():
            src = first_source(piece)
            to_y(src, piece).start()
            to_x(src, piece).start()
            to_s(src, 0, piece).start()
            keep_own(piece).start()

    def column_pass(piece):
        @pl.when(side == 1)
        def _():
            here = place(straight, piece)
            to_y(here, piece).wait_recv()
            to_x(here, piece).start()
            to_s(here, 0, piece).start()

        here = place(cross, piece)
        remote(here, here, x_send.at[piece], x_recv.at[piece], (p, xq)).wait_recv()
        to_s(here, 1, piece).start()

    def column_end(piece):
        for kind in range(2):
            block = (straight, cross)[kind]
            theirs = place(block + 1 - 2 * core, piece)
            remote(
                theirs, theirs, s_send.at[kind, piece], s_recv.at[kind, piece], (p, sq)
            ).wait_recv()
            to_s(theirs, kind, piece).wait_send()
        to_x(place(straight, piece), piece).wait_send()

        @pl.when(side == 0)
        def _():
            to_y(place(straight, piece), piece).wait_send()
            keep_own(piece).wait()

    scatter_part(0, (0, 1, 2))
    scatter_part(1, (0,))
    collect_chunk(0)
    for piece in range(3):
        column_start(piece)
    gather_own(0)
    scatter_part(1, (1, 2))
    column_pass(0)
    gather_pass(0, 1)
    scatter_part(2, (0,))
    column_pass(1)
    gather_pass(0, 2)
    scatter_part(2, (1, 2))
    collect_chunk(1)
    gather_own(1)
    column_pass(2)
    gather_pass(0, 3)
    gather_kept(0)
    column_start(3)
    column_start(4)
    gather_pass(1, 1)
    collect_chunk(2)
    gather_own(2)
    gather_pass(1, 2)
    column_pass(3)
    gather_pass(2, 1)
    gather_pass(1, 3)
    gather_pass(2, 2)
    column_pass(4)
    gather_pass(2, 3)
    gather_kept(1)
    gather_kept(2)
    for c in range(3):
        gather_sent(c)
    for piece in range(5):
        column_end(piece)
    for c in range(3):
        for slot in range(3):
            a2a(c, slot).wait_send()


def exchange(matrix, sending, taking, nrows, width):
    local_rows = nrows * width
    share = local_rows // 4
    dma = pltpu.SemaphoreType.DMA
    vmem = pl.BlockSpec(memory_space=pltpu.VMEM)
    smem = pl.BlockSpec(memory_space=pltpu.SMEM)
    hbm = pl.BlockSpec(memory_space=pl.ANY)
    f32 = jnp.float32
    return pl.pallas_call(
        functools.partial(exchange_kernel, nrows, width),
        out_shape=(
            jax.ShapeDtypeStruct((3, 2 * local_rows, 128), f32),
            jax.ShapeDtypeStruct((3, 8 * width, 128), f32),
            jax.ShapeDtypeStruct((4, 8 * width + 2 * local_rows, 128), f32),
        ),
        in_specs=[smem, smem, vmem],
        out_specs=(vmem, hbm, hbm),
        scratch_shapes=[
            pltpu.VMEM((3, 3, 2 * share, 128), f32),
            pltpu.VMEM((2 * local_rows, 128), f32),
            pltpu.VMEM((2 * local_rows, 128), f32),
            pltpu.VMEM((2 * local_rows, 128), f32),
            dma((3, 3)), dma((3, 3)), dma((3, 2, 4)), dma((3, 2, 4)),
            dma((5,)), dma((5,)), dma((5,)), dma((5,)), dma((2, 5)), dma((2, 5)), dma((8,)),
        ],
        compiler_params=pltpu.CompilerParams(
            collective_id=0, has_side_effects=True, vmem_limit_bytes=60 * 1024 * 1024
        ),
        name="exchange",
    )(sending, taking, matrix)


def halves(x):
    high = x.astype(jnp.bfloat16)
    return high, (x - high.astype(jnp.float32)).astype(jnp.bfloat16)


def left3(x):
    high, rest = halves(x)
    return jnp.concatenate([high, high, rest], axis=1)


def right3(x):
    high, rest = halves(x)
    return jnp.concatenate([high, rest, high], axis=0)


def factor_kernel(
    nrows, width, lower_fill, upper_fill, work_in, tops_in, cols_in, inv, out, l3, u3, c3,
    work, tops, cols, sems,
):
    col_copies = [
        pltpu.make_async_copy(cols_in.at[k], cols.at[k], sems.at[k]) for k in range(4)
    ]
    top_copies = [
        pltpu.make_async_copy(tops_in.at[c], tops.at[c], sems.at[4 + c]) for c in range(3)
    ]
    work_copies = [
        pltpu.make_async_copy(work_in.at[c], work.at[c], sems.at[7 + c]) for c in range(3)
    ]
    for copy in col_copies[:1] + top_copies + col_copies[1:] + work_copies:
        copy.start()
    p = lax.axis_index("prow")
    q = lax.axis_index("pcol")

    def dot(a, b):
        return jnp.dot(a, b, preferred_element_type=jnp.float32)

    def kept(fill, k, block):
        return (block > k) & (fill[k, block] == 1)

    def pairs(ref, lead, start, rows):
        left = ref[lead, pl.ds(start, rows, stride=2), :]
        right = ref[lead, pl.ds(start + 1, rows, stride=2), :]
        return jnp.concatenate([left, right], axis=1)

    corner = 4 * width
    for k in range(4):
        deep = 3 * k * width
        inverse = right3(inv[k])
        col_copies[k].wait()

        def finish(h, start, keep):
            low = jnp.where(keep, dot(left3(h), inverse), 0.0)
            l3[pl.ds(start, width), deep : deep + 3 * width] = left3(low)

        for r in range(4):
            h = pairs(cols, k, 2 * r * width, width)
            take = 3 * min(r, k) * width
            if take:
                h = h - dot(l3[r * width : (r + 1) * width, :take], c3[:take, :])
            if r < k:
                c3[3 * r * width : 3 * (r + 1) * width, :] = right3(
                    jnp.where(kept(upper_fill, r, k), h, 0.0)
                )
            finish(h, r * width, kept(lower_fill, k, r))

        def tile(i, carry):
            start = pl.multiple_of(corner + i * width, width)
            h = pairs(cols, k, 2 * start, width)
            if deep:
                h = h - dot(l3[pl.ds(start, width), :deep], c3[:deep, :])
            finish(h, start, kept(lower_fill, k, i * 4 + p))
            return carry

        lax.fori_loop(0, nrows, tile, 0)
        for c in range(3):
            span = slice(c * width, (c + 1) * width)
            if k == 0:
                top_copies[c].wait()
            u = pairs(tops, c, 2 * k * width, width)
            if deep:
                u = u - dot(l3[k * width : (k + 1) * width, :deep], u3[:deep, span])
            u3[deep : deep + 3 * width, span] = right3(
                jnp.where(kept(upper_fill, k, c * 8 + q), u, 0.0)
            )

    def update(i, carry):
        start = pl.multiple_of(corner + i * width, width)
        for c in range(3):
            span = slice(c * width, (c + 1) * width)
            value = pairs(work, c, 2 * width * i, width) - dot(
                l3[pl.ds(start, width), :], u3[:, span]
            )
            if c == 0:
                for k in range(4):
                    deep = 3 * k * width
                    high = l3[pl.ds(start, width), deep : deep + width].astype(jnp.float32)
                    rest = l3[pl.ds(start, width), deep + 2 * width : deep + 3 * width]
                    low = high + rest.astype(jnp.float32)
                    value = jnp.where((q == k) & (i * 4 + p > k), low, value)
            for half in range(2):
                out[pl.ds(i * (6 * width) + 2 * c + half, width, stride=6), :] = value[
                    :, half * 128 : (half + 1) * 128
                ]
        return carry

    for copy in work_copies:
        copy.wait()
    lax.fori_loop(0, nrows, update, 0)


def factor(lower_fill, upper_fill, work, tops, cols, inverses, nrows, width):
    vmem = pl.BlockSpec(memory_space=pltpu.VMEM)
    smem = pl.BlockSpec(memory_space=pltpu.SMEM)
    rows = (4 + nrows) * width
    bf16 = jnp.bfloat16
    return pl.pallas_call(
        functools.partial(factor_kernel, nrows, width),
        out_shape=jax.ShapeDtypeStruct((nrows * width * 6, 128), jnp.float32),
        in_specs=[smem] * 2 + [pl.BlockSpec(memory_space=pl.ANY)] * 3 + [vmem],
        out_specs=vmem,
        scratch_shapes=[
            pltpu.VMEM((rows, 12 * width), bf16),
            pltpu.VMEM((12 * width, 3 * width), bf16),
            pltpu.VMEM((12 * width, width), bf16),
            pltpu.VMEM(work.shape, jnp.float32),
            pltpu.VMEM(tops.shape, jnp.float32),
            pltpu.VMEM(cols.shape, jnp.float32),
            pltpu.SemaphoreType.DMA((10,)),
        ],
        compiler_params=pltpu.CompilerParams(vmem_limit_bytes=60 * 1024 * 1024),
        name="factor",
    )(lower_fill, upper_fill, work, tops, cols, inverses)


def kernel_body(matrix, row_order, inverses, lower_fill, upper_fill):
    nrows, width = matrix.shape[0], matrix.shape[2]
    p = lax.axis_index("prow")
    sending, taking = index_lists(row_order, nrows, width, 4, p)
    linear = matrix.reshape(nrows * width * 6, 128)
    work, tops, cols = exchange(linear, sending, taking, nrows, width)
    out = factor(lower_fill, upper_fill, work, tops, cols, inverses, nrows, width)
    return out.reshape(matrix.shape)


def solution(mesh):
    in_specs = (P(None, "prow", None, None, "pcol", None), P(), P(), P(), P())
    out_specs = P(None, "prow", None, None, "pcol", None)
    fits = mesh.shape["prow"] == 4 and mesh.shape["pcol"] == 8
    return jax.shard_map(
        kernel_body if fits else body,
        mesh=mesh, in_specs=in_specs, out_specs=out_specs, check_vma=False,
    )
```
